256 devices in a mesh: cohort: 4 (over x), dev: 64 (over z, y, core).
Axes of the slice: x: 4, y: 4, z: 8, core: 2. Of those that a mesh axis runs over, the one named last changes fastest.
Arguments:
- dosage: bfloat16 [524288, 2048], P(('cohort', 'dev')), may hold values from 0 to 2
- allele_freq: float32 [2048], replicated, may hold values from 0.05 to 0.5
- probes: bfloat16 [2048, 512], replicated, may hold values from -6 to 6
- owner_perm: int32 [2048], replicated, may hold values from 0 to 2047, each once
Outputs:
- projected: float32 [2048, 512], P('dev')
The draws below stay inside these ranges and needn't reach their ends.
Inputs may be any that keep to these rules, and one draw needn't show every extreme that they name: `owner_perm`: each SNP appears exactly once.
All inputs are finite; a program needn't handle non-finite values.
Results may differ from the reference program's by a relative error of at most 0.00044.
Values sent between devices are 32-bit elements; how exact they have to be, the bound alone decides.
No kernel may reach another device: no remote copies, remote signals or barrier semaphores. Data moves between devices by JAX's collectives and lax.ppermute only.
A program may use at most 128 MiB of HBM per device.

```python
import jax
import jax.numpy as jnp
from jax import lax

M = 2048
K = 512
SAMPLES = 524288


def block_scale(key, extent, cuts, least, high):
    def one(axis_at, parts):
        draws = jax.random.uniform(jax.random.fold_in(jax.random.fold_in(key, 6), axis_at), (parts,), jnp.float32, least / len(cuts), high / len(cuts))
        return jnp.repeat(jnp.exp(draws), extent[axis_at] // parts).reshape((-1,) + (1,) * (len(extent) - axis_at - 1))

    gain = one(*cuts[0])
    for cut in cuts[1:]:
        gain = gain * one(*cut)
    return gain


def gaussian(rng, extent, width, most, kind=jnp.bfloat16):
    entries = width * jax.random.normal(rng, extent, jnp.float32)
    return jnp.clip(entries, min=-most, max=most).astype(kind)


def setup_inputs(seed: int = 0) -> dict:
    seeds = jax.random.split(jax.random.key(seed), 5)
    dosage = jnp.clip(2.0 * jax.random.uniform(seeds[0], (SAMPLES, M), jnp.float32) ** block_scale(seeds[0], (SAMPLES, M), ((0, 256),), -0.2, 0.2), 0.0, 2.0).astype(jnp.bfloat16)
    allele_freq = jnp.clip(jax.random.uniform(seeds[1], (M,), jnp.float32, 0.05, 0.5), 0.05, 0.5)
    probes = gaussian(seeds[2], (M, K), 1.0, 6.0)
    owner_perm = jax.random.permutation(seeds[3], M).astype(jnp.int32)
    return dict(dosage=dosage, allele_freq=allele_freq, probes=probes, owner_perm=owner_perm)


def reference(dosage, allele_freq, probes, owner_perm):
    mean_dose = 2.0 * allele_freq
    inv_spread = 1.0 / jnp.sqrt(2.0 * allele_freq * (1.0 - allele_freq))
    centered = ((dosage.astype(jnp.float32) - mean_dose[None, :]) * inv_spread[None, :]).astype(jnp.bfloat16)
    sketch = jnp.dot(centered.astype(jnp.float32), probes.astype(jnp.float32), preferred_element_type=jnp.float32)
    gram = jnp.dot(sketch.T, sketch, precision=lax.Precision.HIGHEST)
    lower = jnp.linalg.cholesky(gram)
    basis_t = lax.linalg.triangular_solve(lower, sketch.T, left_side=True, lower=True).astype(jnp.bfloat16)
    full = lax.dot_general(centered.astype(jnp.float32), basis_t.astype(jnp.float32), (((0,), (1,)), ((), ())), preferred_element_type=jnp.float32)
    return jnp.take(full, owner_perm.astype(jnp.int32), axis=0)
```

```python
import jax
import jax.numpy as jnp
from jax import lax
from jax.sharding import Mesh, PartitionSpec as P

NX, NZ, NY, NC = 4, 8, 4, 2
B = 128
NB = 4
PAIRS = [(i, j) for i in range(NB) for j in range(i, NB)]


def shifted(value, axis, size, step):
    return lax.ppermute(value, axis, [(k, (k + step) % size) for k in range(size)])


def spread(value, axes, size):
    return lax.all_to_all(
        jnp.broadcast_to(value[None], (size,) + value.shape), axes, 0, 0, tiled=True
    )


def reduce_gram(packed):
    c = lax.axis_index("c")
    halves = packed.reshape(2, -1, B)
    mine = lax.dynamic_index_in_dim(halves, c, 0, False)
    other = lax.dynamic_index_in_dim(halves, 1 - c, 0, False)
    half = mine + shifted(other, "c", NC, 1)
    part = half.reshape(NX * NY, -1, B)
    part = lax.all_to_all(part, ("x", "y"), 0, 0, tiled=True).sum(0)
    part = spread(part, "z", NZ).sum(0)
    half = spread(part, ("x", "y"), NX * NY).reshape(-1, B)
    other = shifted(half, "c", NC, 1)
    first = jnp.where(c == 0, half, other)
    second = jnp.where(c == 0, other, half)
    return jnp.concatenate([first, second], axis=0)


def row_order(owner_perm):
    x, z, y, c = (lax.axis_index(a) for a in ("x", "z", "y", "c"))
    ci, yi, zi, r = jnp.ix_(jnp.arange(NC), jnp.arange(NY), jnp.arange(NZ), jnp.arange(32))
    row = 32 * (zi * (NY * NC) + ((y + yi) % NY) * NC + (c + ci) % NC) + r
    return jnp.take(owner_perm, row.reshape(-1), axis=0)


def reduce_product(rows):
    k = rows.shape[1]
    part = rows.reshape(NC, -1, k)
    part = part[0] + shifted(part[1], "c", NC, 1)
    part = part.reshape(NY, -1, k)
    total = part[0]
    for s in range(1, NY):
        total = total + shifted(part[s], "y", NY, s)
    part = total.reshape(NZ, -1, k)
    part = lax.all_to_all(part, "z", 0, 0, tiled=True).sum(0)
    total = part
    for s in range(1, NX):
        total = total + shifted(part, "x", NX, s)
    return total


def body(dosage, allele_freq, probes, owner_perm):
    mean_dose = 2.0 * allele_freq
    inv_spread = 1.0 / jnp.sqrt(2.0 * allele_freq * (1.0 - allele_freq))
    centered = ((dosage.astype(jnp.float32) - mean_dose[None, :]) * inv_spread[None, :]).astype(
        jnp.bfloat16
    )
    sketch = jnp.dot(centered, probes, preferred_element_type=jnp.float32)
    blocks = []
    for i, j in PAIRS:
        blocks.append(
            lax.dot_general(
                sketch[:, i * B : (i + 1) * B],
                sketch[:, j * B : (j + 1) * B],
                (((0,), (0,)), ((), ())),
                precision=lax.Precision.HIGHEST,
            )
        )
    gram_blocks = reduce_gram(jnp.concatenate(blocks, axis=0)).reshape(-1, B, B)
    high = sketch.astype(jnp.bfloat16)
    low = (sketch - high.astype(jnp.float32)).astype(jnp.bfloat16)
    product = lax.dot_general(
        centered, high, (((0,), (0,)), ((), ())), preferred_element_type=jnp.float32
    ) + lax.dot_general(
        centered, low, (((0,), (0,)), ((), ())), preferred_element_type=jnp.float32
    )
    owned = reduce_product(jnp.take(product, row_order(owner_perm), axis=0))
    at = {pair: gram_blocks[n] for n, pair in enumerate(PAIRS)}
    gram = jnp.concatenate(
        [
            jnp.concatenate(
                [at[i, j] if i <= j else at[j, i].T for j in range(NB)], axis=1
            )
            for i in range(NB)
        ],
        axis=0,
    )
    lower = jnp.linalg.cholesky(gram)
    return lax.linalg.triangular_solve(lower, owned.T, left_side=True, lower=True).T


def solution(mesh):
    torus = Mesh(mesh.devices.reshape(NX, NZ, NY, NC), ("x", "z", "y", "c"))
    return jax.shard_map(
        body,
        mesh=torus,
        in_specs=(P(("x", "z", "y", "c"), None), P(), P(), P()),
        out_specs=P(("z", "y", "c"), None),
        check_vma=False,
    )
```

```python
import functools

import jax
import jax.numpy as jnp
from jax import lax
from jax.experimental import pallas as pl
from jax.experimental.pallas import tpu as pltpu
from jax.sharding import Mesh, PartitionSpec as P


NX, NZ, NY, NC = 4, 8, 4, 2
B = 128
NB = 4
PAIRS = [(i, j) for i in range(NB) for j in range(i, NB)]
TN = (((0,), (0,)), ((), ()))


def dot(a, b, dims):
    return lax.dot_general(a, b, dims, preferred_element_type=jnp.float32)


def sketch_kernel(d_ref, m_ref, s_ref, p_ref, hi_ref, lo_ref, g_ref):
    c = ((d_ref[...].astype(jnp.float32) - m_ref[...]) * s_ref[...]).astype(jnp.bfloat16)
    sketch = jnp.dot(c, p_ref[...], preferred_element_type=jnp.float32)
    hi = sketch.astype(jnp.bfloat16)
    lo = (sketch - hi.astype(jnp.float32)).astype(jnp.bfloat16)
    hi_ref[...] = hi
    lo_ref[...] = lo
    first = pl.program_id(0) == 0
    for p in range(NB):
        a, b = slice(p * B, (p + 1) * B), slice(p * B, None)
        strip = dot(hi[:, a], hi[:, b], TN) + dot(hi[:, a], lo[:, b], TN) + dot(lo[:, a], hi[:, b], TN)
        for t in range(NB - p):
            n = PAIRS.index((p, p + t))
            at = slice(n * B, (n + 1) * B)
            piece = strip[:, t * B : (t + 1) * B]

            @pl.when(first)
            def _():
                g_ref[at, :] = piece

            @pl.when(jnp.logical_not(first))
            def _():
                g_ref[at, :] += piece


def sketch_gram(dosage, mean, scale, probes, step=1024):
    n, m = dosage.shape
    k = probes.shape[1]
    whole = lambda i: (0, 0)
    return pl.pallas_call(
        sketch_kernel,
        grid=(n // step,),
        in_specs=[
            pl.BlockSpec((step, m), lambda i: (i, 0)),
            pl.BlockSpec((1, m), whole),
            pl.BlockSpec((1, m), whole),
            pl.BlockSpec((m, k), whole),
        ],
        out_specs=(
            pl.BlockSpec((step, k), lambda i: (i, 0)),
            pl.BlockSpec((step, k), lambda i: (i, 0)),
            pl.BlockSpec((len(PAIRS) * B, B), whole),
        ),
        out_shape=(
            jax.ShapeDtypeStruct((n, k), jnp.bfloat16),
            jax.ShapeDtypeStruct((n, k), jnp.bfloat16),
            jax.ShapeDtypeStruct((len(PAIRS) * B, B), jnp.float32),
        ),
        name="sketch_gram",
    )(dosage, mean, scale, probes)


def product_kernel(d_ref, m_ref, s_ref, hi_ref, lo_ref, w_ref):
    c = ((d_ref[...].astype(jnp.float32) - m_ref[...]) * s_ref[...]).astype(jnp.bfloat16)
    w_ref[...] = dot(c, hi_ref[...], TN) + dot(c, lo_ref[...], TN)


def product(dosage, mean, scale, hi, lo, step=256):
    n, m = dosage.shape
    k = hi.shape[1]
    whole = lambda i: (0, 0)
    return pl.pallas_call(
        product_kernel,
        grid=(m // step,),
        in_specs=[
            pl.BlockSpec((n, step), lambda i: (0, i)),
            pl.BlockSpec((1, step), lambda i: (0, i)),
            pl.BlockSpec((1, step), lambda i: (0, i)),
            pl.BlockSpec((n, k), whole),
            pl.BlockSpec((n, k), whole),
        ],
        out_specs=pl.BlockSpec((step, k), lambda i: (i, 0)),
        out_shape=jax.ShapeDtypeStruct((m, k), jnp.float32),
        name="product",
    )(dosage, mean, scale, hi, lo)


def gather_kernel(i_ref, w_ref, o_ref):
    def eight(r, _):
        base = pl.multiple_of(r * 8, 8)
        o_ref[pl.ds(base, 8), :] = jnp.concatenate(
            [w_ref[pl.ds(i_ref[base + s], 1), :] for s in range(8)], axis=0)
        return 0

    lax.fori_loop(0, o_ref.shape[0] // 8, eight, 0, unroll=2)


def gather_rows(index, rows):
    return pl.pallas_call(
        gather_kernel,
        out_shape=jax.ShapeDtypeStruct((index.shape[0], rows.shape[1]), rows.dtype),
        in_specs=[pl.BlockSpec(memory_space=pltpu.SMEM), pl.BlockSpec(memory_space=pltpu.VMEM)],
        out_specs=pl.BlockSpec(memory_space=pltpu.VMEM),
        name="gather_rows",
    )(index, rows)


HI = lax.Precision.HIGHEST
NT = (((1,), (1,)), ((), ()))


def factor_kernel(p, g_ref, *refs):
    prior = refs[:p]
    r_ref, inv_ref, s_ref = refs[p:]
    w = (NB - p) * B
    wide = w + B
    for t in range(NB - p):
        n = PAIRS.index((p, p + t))
        s_ref[:, t * B : (t + 1) * B] = g_ref[n * B : (n + 1) * B, :]
    for q in range(p):
        off = (p - q) * B
        s_ref[:, :w] -= lax.dot_general(
            prior[q][:, off : off + B], prior[q][:, off:], TN,
            precision=HI, preferred_element_type=jnp.float32)
    s_ref[:, w:] = (
        lax.broadcasted_iota(jnp.int32, (B, B), 0) == lax.broadcasted_iota(jnp.int32, (B, B), 1)
    ).astype(jnp.float32)
    for b in range(B // 8):
        lo = 8 * b
        rows = s_ref[lo : lo + 8, :]
        cols = [jnp.broadcast_to(rows[:, lo + m : lo + m + 1], (8, B)) for m in range(8)]
        e = [[jnp.broadcast_to(cols[m][j : j + 1, :], (8, B)) if j >= m else None
              for m in range(8)] for j in range(8)]
        u = [[jnp.broadcast_to(rows[j : j + 1, t * B : (t + 1) * B], (8, B))
              for t in range(wide // B)] for j in range(8)]
        inv = [None] * 8
        l = [[None] * 8 for _ in range(8)]
        for j in range(8):
            inv[j] = 1.0 / e[j][j]
            for m in range(j + 1, 8):
                l[m][j] = e[m][j] * inv[j]
            for m in range(j + 1, 8):
                for n in range(m, 8):
                    e[n][m] = e[n][m] - l[n][j] * e[m][j]
                u[m] = [a - l[m][j] * c for a, c in zip(u[m], u[j])]
        v = [[a * inv[j] for a in u[j]] for j in range(8)]
        for j in range(8):
            root = lax.rsqrt(e[j][j])
            root = root * (1.5 - 0.5 * e[j][j] * root * root)
            for t in range(wide // B):
                row = (u[j][t] * root)[0:1, :]
                if t < NB - p:
                    r_ref[lo + j : lo + j + 1, t * B : (t + 1) * B] = row
                else:
                    inv_ref[lo + j : lo + j + 1, :] = row
        for d in range(b + 1, B // 8):
            at = slice(8 * d, 8 * d + 8)
            tail = s_ref[at, :]
            cols = [jnp.broadcast_to(tail[:, lo + m : lo + m + 1], (8, B)) for m in range(8)]
            for j in range(8):
                for m in range(j + 1, 8):
                    cols[m] = cols[m] - cols[j] * l[m][j]
            for t in range(wide // B):
                x = tail[:, t * B : (t + 1) * B]
                y = cols[0] * v[0][t]
                z = cols[1] * v[1][t]
                for m in range(2, 8, 2):
                    y = y + cols[m] * v[m][t]
                    z = z + cols[m + 1] * v[m + 1][t]
                s_ref[at, t * B : (t + 1) * B] = x - (y + z)


def factor(p, packed, prior):
    w = (NB - p) * B
    vm = pl.BlockSpec(memory_space=pltpu.VMEM)
    return pl.pallas_call(
        functools.partial(factor_kernel, p),
        out_shape=(
            jax.ShapeDtypeStruct((B, w), jnp.float32),
            jax.ShapeDtypeStruct((B, B), jnp.float32),
        ),
        in_specs=[vm] * (1 + p),
        out_specs=(vm, vm),
        scratch_shapes=[pltpu.VMEM((B, w + B), jnp.float32)],
        cost_estimate=pl.CostEstimate(flops=10_000_000_000, bytes_accessed=1 << 20, transcendentals=0),
    )(packed, *prior)


def finish_kernel(w_ref, *refs):
    r, inv, x_ref = refs[:NB], refs[NB : 2 * NB], refs[2 * NB]
    for p in range(NB):
        acc = w_ref[:, p * B : (p + 1) * B]
        for q in range(p):
            acc = acc - lax.dot_general(
                x_ref[:, q * B : (q + 1) * B], r[q][:, (p - q) * B : (p - q + 1) * B],
                (((1,), (0,)), ((), ())), precision=HI, preferred_element_type=jnp.float32)
        x_ref[:, p * B : (p + 1) * B] = lax.dot_general(
            acc, inv[p][...], NT, precision=HI, preferred_element_type=jnp.float32)


def finish(owned, panels, inverses):
    vm = pl.BlockSpec(memory_space=pltpu.VMEM)
    return pl.pallas_call(
        finish_kernel,
        out_shape=jax.ShapeDtypeStruct(owned.shape, jnp.float32),
        in_specs=[vm] * (1 + 2 * NB),
        out_specs=vm,
        name="finish",
    )(owned, *panels, *inverses)


def shifted(value, axis, size, step):
    return lax.ppermute(value, axis, [(k, (k + step) % size) for k in range(size)])


def exchange(value, axis, size):
    total = value
    for s in range(1, size):
        total = total + shifted(value, axis, size, s)
    return total


def after(value, *others):
    return lax.optimization_barrier((value,) + others)


def row_order(owner_perm):
    _, _, y, c = (lax.axis_index(a) for a in ("x", "z", "y", "c"))
    ci, yi, zi, r = jnp.ix_(jnp.arange(NC), jnp.arange(NY), jnp.arange(NZ), jnp.arange(32))
    row = 32 * (zi * (NY * NC) + ((y + yi) % NY) * NC + (c + ci) % NC) + r
    return owner_perm.at[row.reshape(-1)].get(mode="promise_in_bounds")


def steps(dosage, allele_freq, probes, owner_perm):
    c = lax.axis_index("c")
    mean_dose = (2.0 * allele_freq)[None, :]
    inv_spread = (1.0 / jnp.sqrt(2.0 * allele_freq * (1.0 - allele_freq)))[None, :]
    order = row_order(owner_perm)
    high, low, packed = sketch_gram(dosage, mean_dose, inv_spread, probes)
    packed, order = after(packed, order)
    halves = packed.reshape(NC, -1, B)
    mine = lax.dynamic_index_in_dim(halves, c, 0, False)
    other = lax.dynamic_index_in_dim(halves, 1 - c, 0, False)
    half = mine + shifted(other, "c", NC, 1)
    half, high = after(half, high)
    part = half.reshape(NX * NZ, -1, B)
    part = lax.all_to_all(part, ("x", "z"), 0, 0, tiled=True)
    rows = product(dosage, mean_dose, inv_spread, high, low)
    part = part.sum(0)
    part, rows = after(part, rows)
    total = exchange(part, "y", NY)
    away = gather_rows(order[1024:], rows)
    total, away, rows = after(total, away, rows)
    came = shifted(away, "c", NC, 1)
    spread = jnp.broadcast_to(total[None], (NX * NZ,) + total.shape)
    half = lax.all_to_all(spread, ("x", "z"), 0, 0, tiled=True).reshape(-1, B)
    kept = gather_rows(order[:1024], rows)
    half, kept, came = after(half, kept, came)
    other = shifted(half, "c", NC, 1)
    packed = jnp.concatenate(
        [jnp.where(c == 0, half, other), jnp.where(c == 0, other, half)], axis=0
    )
    k = rows.shape[1]
    packed, block = after(packed, (kept + came).reshape(NY, -1, k))
    sent = []
    for s in range(1, NY):
        sent.append(shifted(block[s], "y", NY, s))
    panels, inverses = [], []
    for p in range(NB):
        r, inv = factor(p, packed, panels)
        panels.append(r)
        inverses.append(inv)
    owned = block[0]
    for part in sent:
        owned = owned + part
    owned = lax.all_to_all(owned.reshape(NZ, -1, k), "z", 0, 0, tiled=True)
    owned = exchange(owned.sum(0), "x", NX)
    return finish(owned, panels, inverses)


def solution(mesh):
    torus = Mesh(mesh.devices.reshape(NX, NZ, NY, NC), ("x", "z", "y", "c"))
    return jax.shard_map(
        steps,
        mesh=torus,
        in_specs=(P(("x", "z", "y", "c"), None), P(), P(), P()),
        out_specs=P(("z", "y", "c"), None),
        check_vma=False,
    )
```

```python
import functools

import jax
import jax.numpy as jnp
from jax import lax
from jax.experimental import pallas as pl
from jax.experimental.pallas import tpu as pltpu
from jax.sharding import Mesh, PartitionSpec as P


NX, NZ, NY, NC = 4, 8, 4, 2
B = 128
NB = 4
PAIRS = [(i, j) for i in range(NB) for j in range(i, NB)]
HALF = len(PAIRS) // 2

TN = (((0,), (0,)), ((), ()))


def dot(a, b, dims):
    return lax.dot_general(a, b, dims, preferred_element_type=jnp.float32)


def sketch_kernel(me_ref, d_ref, m_ref, s_ref, p_ref, hl_ref, g_ref, a_ref):
    k = p_ref.shape[1]
    c = ((d_ref[...].astype(jnp.float32) - m_ref[...]) * s_ref[...]).astype(jnp.bfloat16)
    sketch = jnp.dot(c, p_ref[...], preferred_element_type=jnp.float32)
    hi = sketch.astype(jnp.bfloat16)
    lo = (sketch - hi.astype(jnp.float32)).astype(jnp.bfloat16)
    hl_ref[:, :k] = hi
    hl_ref[:, k:] = lo
    i = pl.program_id(0)

    @pl.when(i == 0)
    def _():
        a_ref[...] = dot(hi, hl_ref[...], TN)

    @pl.when(i > 0)
    def _():
        a_ref[...] += dot(hi, hl_ref[...], TN)

    @pl.when(i == pl.num_programs(0) - 1)
    def _():
        for n, (p, q) in enumerate(PAIRS):
            r, t = slice(p * B, (p + 1) * B), slice(q * B, (q + 1) * B)
            u, v = slice(k + p * B, k + (p + 1) * B), slice(k + q * B, k + (q + 1) * B)
            side = (n // HALF + me_ref[0]) & 1
            g_ref[side, n % HALF * B : (n % HALF + 1) * B, :] = a_ref[r, t] + (a_ref[r, v] + a_ref[t, u].T)


def sketch_gram(me, dosage, mean, scale, probes, step=512):
    n, m = dosage.shape
    k = probes.shape[1]
    whole = lambda i: (0, 0)
    return pl.pallas_call(
        sketch_kernel,
        grid=(n // step,),
        in_specs=[
            pl.BlockSpec(memory_space=pltpu.SMEM),
            pl.BlockSpec((step, m), lambda i: (i, 0)),
            pl.BlockSpec((1, m), whole),
            pl.BlockSpec((1, m), whole),
            pl.BlockSpec((m, k), whole),
        ],
        out_specs=(
            pl.BlockSpec((step, 2 * k), lambda i: (i, 0)),
            pl.BlockSpec((NC, HALF * B, B), lambda i: (0, 0, 0)),
        ),
        out_shape=(
            jax.ShapeDtypeStruct((n, 2 * k), jnp.bfloat16),
            jax.ShapeDtypeStruct((NC, HALF * B, B), jnp.float32),
        ),
        scratch_shapes=[pltpu.VMEM((k, 2 * k), jnp.float32)],
        name="sketch_gram",
    )(me, dosage, mean, scale, probes)


def product_kernel(d_ref, m_ref, s_ref, hl_ref, *refs):
    w_ref = refs[-1]
    k = w_ref.shape[1]
    c = ((d_ref[...].astype(jnp.float32) - m_ref[...]) * s_ref[...]).astype(jnp.bfloat16)
    both = dot(c, hl_ref[...], TN)
    w_ref[...] = both[:, :k] + both[:, k:]


def product(part, dosage, mean, scale, hl, *earlier, step=512):
    n, m = dosage.shape
    k = hl.shape[1] // 2
    steps = m // step // 2
    off = part * steps
    return pl.pallas_call(
        product_kernel,
        grid=(steps,),
        in_specs=[
            pl.BlockSpec((n, step), lambda i: (0, i + off)),
            pl.BlockSpec((1, step), lambda i: (0, i + off)),
            pl.BlockSpec((1, step), lambda i: (0, i + off)),
            pl.BlockSpec((n, 2 * k), lambda i: (0, 0)),
        ]
        + [pl.BlockSpec(memory_space=pl.ANY)] * part,
        out_specs=pl.BlockSpec((step, k), lambda i: (i + off, 0)),
        out_shape=jax.ShapeDtypeStruct((m, k), jnp.float32),
        input_output_aliases={4: 0} if part else {},
        cost_estimate=pl.CostEstimate(
            flops=2 * n * m * k, bytes_accessed=12 << 20, transcendentals=0
        ),
    )(dosage, mean, scale, hl, *earlier)


def gather_kernel(flip, me_ref, i_ref, w_ref, *refs):
    o_ref = refs[-1]
    c = (me_ref[0] + flip) & 1

    def block(n, _):
        base = 32 * ((n & 7) * (NY * NC) + ((n >> 3) & 3) * NC + c) + 8 * (n >> 5)
        at = pl.ds(pl.multiple_of(n * 8, 8), 8)
        rows = jnp.concatenate([w_ref[pl.ds(i_ref[base + s], 1), :] for s in range(8)], axis=0)
        o_ref[at, :] = rows if flip else rows + refs[0][at, :]
        return 0

    lax.fori_loop(0, NX * NY * NZ, block, 0, unroll=4)


def gather_rows(flip, me, perm, rows, *came):
    sm, vm = pl.BlockSpec(memory_space=pltpu.SMEM), pl.BlockSpec(memory_space=pltpu.VMEM)
    return pl.pallas_call(
        functools.partial(gather_kernel, flip),
        out_shape=jax.ShapeDtypeStruct((rows.shape[0] // NC, rows.shape[1]), rows.dtype),
        in_specs=[sm, sm, vm] + [vm] * len(came),
        out_specs=vm,
        cost_estimate=pl.CostEstimate(flops=6_000_000_000, bytes_accessed=8 << 20, transcendentals=0),
    )(me, perm, rows, *came)


HI = lax.Precision.HIGHEST
NT = (((1,), (1,)), ((), ()))


def factor_kernel(p, me_ref, near_ref, far_ref, *refs):
    prior = refs[:p]
    r_ref, inv_ref, s_ref = refs[p:]
    w = (NB - p) * B
    wide = w + B
    for t in range(NB - p):
        n = PAIRS.index((p, p + t))
        at = slice(n % HALF * B, (n % HALF + 1) * B)
        near = (n // HALF + me_ref[0]) & 1 == 0
        s_ref[:, t * B : (t + 1) * B] = jnp.where(near, near_ref[at, :], far_ref[at, :])
    for q in range(p):
        off = (p - q) * B
        s_ref[:, :w] -= lax.dot_general(
            prior[q][:, off : off + B], prior[q][:, off:], TN,
            precision=HI, preferred_element_type=jnp.float32)
    s_ref[:, w:] = (
        lax.broadcasted_iota(jnp.int32, (B, B), 0) == lax.broadcasted_iota(jnp.int32, (B, B), 1)
    ).astype(jnp.float32)
    for b in range(B // 8):
        lo = 8 * b
        rows = s_ref[lo : lo + 8, :]
        cols = [jnp.broadcast_to(rows[:, lo + m : lo + m + 1], (8, B)) for m in range(8)]
        e = [[jnp.broadcast_to(cols[m][j : j + 1, :], (8, B)) if j >= m else None
              for m in range(8)] for j in range(8)]
        u = [[jnp.broadcast_to(rows[j : j + 1, t * B : (t + 1) * B], (8, B))
              for t in range(wide // B)] for j in range(8)]
        inv = [None] * 8
        l = [[None] * 8 for _ in range(8)]
        for j in range(8):
            inv[j] = 1.0 / e[j][j]
            for m in range(j + 1, 8):
                l[m][j] = e[m][j] * inv[j]
            for m in range(j + 1, 8):
                for n in range(m, 8):
                    e[n][m] = e[n][m] - l[n][j] * e[m][j]
                u[m] = [a - l[m][j] * c for a, c in zip(u[m], u[j])]
        v = [[a * inv[j] for a in u[j]] for j in range(8)]
        for j in range(8):
            root = lax.rsqrt(e[j][j])
            root = root * (1.5 - 0.5 * e[j][j] * root * root)
            for t in range(wide // B):
                row = (u[j][t] * root)[0:1, :]
                if t < NB - p:
                    r_ref[lo + j : lo + j + 1, t * B : (t + 1) * B] = row
                else:
                    inv_ref[lo + j : lo + j + 1, :] = row
        for d in range(b + 1, B // 8):
            at = slice(8 * d, 8 * d + 8)
            tail = s_ref[at, :]
            cols = [jnp.broadcast_to(tail[:, lo + m : lo + m + 1], (8, B)) for m in range(8)]
            for j in range(8):
                for m in range(j + 1, 8):
                    cols[m] = cols[m] - cols[j] * l[m][j]
            for t in range(wide // B):
                x = tail[:, t * B : (t + 1) * B]
                y = cols[0] * v[0][t]
                z = cols[1] * v[1][t]
                for m in range(2, 8, 2):
                    y = y + cols[m] * v[m][t]
                    z = z + cols[m + 1] * v[m + 1][t]
                s_ref[at, t * B : (t + 1) * B] = x - (y + z)


def factor(p, me, near, far, prior):
    w = (NB - p) * B
    vm = pl.BlockSpec(memory_space=pltpu.VMEM)
    return pl.pallas_call(
        functools.partial(factor_kernel, p),
        out_shape=(
            jax.ShapeDtypeStruct((B, w), jnp.float32),
            jax.ShapeDtypeStruct((B, B), jnp.float32),
        ),
        in_specs=[pl.BlockSpec(memory_space=pltpu.SMEM)] + [vm] * (2 + p),
        out_specs=(vm, vm),
        scratch_shapes=[pltpu.VMEM((B, w + B), jnp.float32)],
        cost_estimate=pl.CostEstimate(flops=10_000_000_000, bytes_accessed=1 << 20, transcendentals=0),
    )(me, near, far, *prior)


def finish_kernel(w_ref, *refs):
    r, inv, x_ref = refs[:NB], refs[NB : 2 * NB], refs[2 * NB]
    for p in range(NB):
        acc = w_ref[:, p * B : (p + 1) * B]
        for q in range(p):
            acc = acc - lax.dot_general(
                x_ref[:, q * B : (q + 1) * B], r[q][:, (p - q) * B : (p - q + 1) * B],
                (((1,), (0,)), ((), ())), precision=HI, preferred_element_type=jnp.float32)
        x_ref[:, p * B : (p + 1) * B] = lax.dot_general(
            acc, inv[p][...], NT, precision=HI, preferred_element_type=jnp.float32)


def finish(owned, panels, inverses):
    vm = pl.BlockSpec(memory_space=pltpu.VMEM)
    return pl.pallas_call(
        finish_kernel,
        out_shape=jax.ShapeDtypeStruct(owned.shape, jnp.float32),
        in_specs=[vm] * (1 + 2 * NB),
        out_specs=vm,
        name="finish",
    )(owned, *panels, *inverses)


def shifted(value, axis, size, step):
    return lax.ppermute(value, axis, [(k, (k + step) % size) for k in range(size)])


def swap(value, axes):
    return lax.all_to_all(value, axes, 0, 0, tiled=True)


def copies(value, count):
    return jnp.broadcast_to(value[None], (count,) + value.shape)


def after(value, *others):
    return lax.optimization_barrier((value,) + others)


def steps(dosage, allele_freq, probes, owner_perm):
    c = lax.axis_index("c")
    me = jnp.full((1,), c, jnp.int32)
    mean_dose = (2.0 * allele_freq)[None, :]
    inv_spread = (1.0 / jnp.sqrt(2.0 * allele_freq * (1.0 - allele_freq)))[None, :]
    both, packed = sketch_gram(me, dosage, mean_dose, inv_spread, probes)
    half = packed[0] + shifted(packed[1], "c", NC, 1)
    half, both = after(half, both)
    part = swap(half.reshape(NX * NY, -1, B), ("x", "y"))
    rows = product(0, dosage, mean_dose, inv_spread, both)
    part, rows = after(part.sum(0), rows)
    part = swap(copies(part, NZ), "z")
    rows = product(1, dosage, mean_dose, inv_spread, both, rows)
    part, rows = after(part.sum(0), rows)
    near = swap(copies(part, NX * NY), ("x", "y")).reshape(-1, B)
    away = gather_rows(1, me, owner_perm, rows)
    near, away = after(near, away)
    far = shifted(near, "c", NC, 1)
    came = shifted(away, "c", NC, 1)
    kept = gather_rows(0, me, owner_perm, rows, came)
    k = rows.shape[1]
    near, kept = after(near, kept)
    owned = swap(kept.reshape(NX * NY, -1, k), ("x", "y"))
    panels, inverses = [], []
    for p in range(NB):
        r, inv = factor(p, me, near, far, panels)
        panels.append(r)
        inverses.append(inv)
    owned = owned.sum(0).reshape(NZ, -1, k)
    owned = swap(copies(owned, NX).reshape(NX * NZ, -1, k), ("x", "z"))
    owned = owned.reshape(NX, NZ, -1, k).sum(1).reshape(-1, k)
    return finish(owned, panels, inverses)


def solution(mesh):
    torus = Mesh(mesh.devices.reshape(NX, NZ, NY, NC), ("x", "z", "y", "c"))
    return jax.shard_map(
        steps,
        mesh=torus,
        in_specs=(P(("x", "z", "y", "c"), None), P(), P(), P()),
        out_specs=P(("z", "y", "c"), None),
        check_vma=False,
    )
```

```python
import functools

import jax
import jax.numpy as jnp
from jax import lax
from jax.experimental import pallas as pl
from jax.experimental.pallas import tpu as pltpu
from jax.sharding import Mesh, PartitionSpec as P


NX, NZ, NY, NC = 4, 8, 4, 2
B = 128
NB = 4
PAIRS = [(i, j) for i in range(NB) for j in range(i, NB)]
HALF = len(PAIRS) // 2

TN = (((0,), (0,)), ((), ()))


def dot(a, b, dims):
    return lax.dot_general(a, b, dims, preferred_element_type=jnp.float32)


def sketch_kernel(me_ref, d_ref, m_ref, s_ref, p_ref, hl_ref, near_ref, far_ref, a_ref):
    k = p_ref.shape[1]
    c = ((d_ref[...].astype(jnp.float32) - m_ref[...]) * s_ref[...]).astype(jnp.bfloat16)
    sketch = jnp.dot(c, p_ref[...], preferred_element_type=jnp.float32)
    hi = sketch.astype(jnp.bfloat16)
    lo = (sketch - hi.astype(jnp.float32)).astype(jnp.bfloat16)
    hl_ref[:, :k] = hi
    hl_ref[:, k:] = lo
    i = pl.program_id(0)

    @pl.when(i == 0)
    def _():
        a_ref[...] = dot(hi, hl_ref[...], TN)

    @pl.when(i > 0)
    def _():
        a_ref[...] += dot(hi, hl_ref[...], TN)

    @pl.when(i == pl.num_programs(0) - 1)
    def _():
        def block(p, q):
            r, t = slice(p * B, (p + 1) * B), slice(q * B, (q + 1) * B)
            u, v = slice(k + p * B, k + (p + 1) * B), slice(k + q * B, k + (q + 1) * B)
            return a_ref[r, t] + (a_ref[r, v] + a_ref[t, u].T)

        first = me_ref[0] == 0
        for n in range(HALF):
            at = slice(n * B, (n + 1) * B)
            a, b = block(*PAIRS[n]), block(*PAIRS[n + HALF])
            near_ref[at, :] = jnp.where(first, a, b)
            far_ref[at, :] = jnp.where(first, b, a)


def sketch_gram(me, dosage, mean, scale, probes, step=512):
    n, m = dosage.shape
    k = probes.shape[1]
    whole = lambda i: (0, 0)
    return pl.pallas_call(
        sketch_kernel,
        grid=(n // step,),
        in_specs=[
            pl.BlockSpec(memory_space=pltpu.SMEM),
            pl.BlockSpec((step, m), lambda i: (i, 0)),
            pl.BlockSpec((1, m), whole),
            pl.BlockSpec((1, m), whole),
            pl.BlockSpec((m, k), whole),
        ],
        out_specs=(
            pl.BlockSpec((step, 2 * k), lambda i: (i, 0)),
            pl.BlockSpec((HALF * B, B), whole),
            pl.BlockSpec((HALF * B, B), whole),
        ),
        out_shape=(
            jax.ShapeDtypeStruct((n, 2 * k), jnp.bfloat16),
            jax.ShapeDtypeStruct((HALF * B, B), jnp.float32),
            jax.ShapeDtypeStruct((HALF * B, B), jnp.float32),
        ),
        scratch_shapes=[pltpu.VMEM((k, 2 * k), jnp.float32)],
        name="sketch_gram",
    )(me, dosage, mean, scale, probes)


def product_kernel(d_ref, m_ref, s_ref, hl_ref, w_ref):
    k = w_ref.shape[1]
    c = ((d_ref[...].astype(jnp.float32) - m_ref[...]) * s_ref[...]).astype(jnp.bfloat16)
    both = dot(c, hl_ref[...], TN)
    w_ref[...] = both[:, :k] + both[:, k:]


def product(dosage, mean, scale, hl, step=512):
    n, m = dosage.shape
    k = hl.shape[1] // 2
    return pl.pallas_call(
        product_kernel,
        grid=(m // step,),
        in_specs=[
            pl.BlockSpec((n, step), lambda i: (0, i)),
            pl.BlockSpec((1, step), lambda i: (0, i)),
            pl.BlockSpec((1, step), lambda i: (0, i)),
            pl.BlockSpec((n, 2 * k), lambda i: (0, 0)),
        ],
        out_specs=pl.BlockSpec((step, k), lambda i: (i, 0)),
        out_shape=jax.ShapeDtypeStruct((m, k), jnp.float32),
        name="product",
        cost_estimate=pl.CostEstimate(
            flops=4 * n * m * k, bytes_accessed=16 << 20, transcendentals=0
        ),
    )(dosage, mean, scale, hl)


def gather_kernel(flip, me_ref, i_ref, w_ref, *refs):
    o_ref = refs[-1]
    c = (me_ref[0] + flip) & 1

    def block(n, _):
        base = 32 * ((n & 7) * (NY * NC) + ((n >> 3) & 3) * NC + c) + 8 * (n >> 5)
        at = pl.ds(pl.multiple_of(n * 8, 8), 8)
        rows = jnp.concatenate([w_ref[pl.ds(i_ref[base + s], 1), :] for s in range(8)], axis=0)
        o_ref[at, :] = rows if flip else rows + refs[0][at, :]
        return 0

    lax.fori_loop(0, NX * NY * NZ, block, 0, unroll=4)


def gather_rows(flip, me, perm, rows, *came):
    sm, vm = pl.BlockSpec(memory_space=pltpu.SMEM), pl.BlockSpec(memory_space=pltpu.VMEM)
    return pl.pallas_call(
        functools.partial(gather_kernel, flip),
        out_shape=jax.ShapeDtypeStruct((rows.shape[0] // NC, rows.shape[1]), rows.dtype),
        in_specs=[sm, sm, vm] + [vm] * len(came),
        out_specs=vm,
        cost_estimate=pl.CostEstimate(flops=6_000_000_000, bytes_accessed=8 << 20, transcendentals=0),
    )(me, perm, rows, *came)


HI = lax.Precision.HIGHEST
NT = (((1,), (1,)), ((), ()))


def factor_kernel(p, me_ref, near_ref, far_ref, *refs):
    prior = refs[:p]
    r_ref, inv_ref, s_ref = refs[p:]
    w = (NB - p) * B
    wide = w + B
    for t in range(NB - p):
        n = PAIRS.index((p, p + t))
        at = slice(n % HALF * B, (n % HALF + 1) * B)
        near = (n // HALF + me_ref[0]) & 1 == 0
        s_ref[:, t * B : (t + 1) * B] = jnp.where(near, near_ref[at, :], far_ref[at, :])
    for q in range(p):
        off = (p - q) * B
        s_ref[:, :w] -= lax.dot_general(
            prior[q][:, off : off + B], prior[q][:, off:], TN,
            precision=HI, preferred_element_type=jnp.float32)
    s_ref[:, w:] = (
        lax.broadcasted_iota(jnp.int32, (B, B), 0) == lax.broadcasted_iota(jnp.int32, (B, B), 1)
    ).astype(jnp.float32)
    for b in range(B // 8):
        lo = 8 * b
        rows = s_ref[lo : lo + 8, :]
        cols = [jnp.broadcast_to(rows[:, lo + m : lo + m + 1], (8, B)) for m in range(8)]
        e = [[jnp.broadcast_to(cols[m][j : j + 1, :], (8, B)) if j >= m else None
              for m in range(8)] for j in range(8)]
        u = [[jnp.broadcast_to(rows[j : j + 1, t * B : (t + 1) * B], (8, B))
              for t in range(wide // B)] for j in range(8)]
        inv = [None] * 8
        l = [[None] * 8 for _ in range(8)]
        for j in range(8):
            inv[j] = 1.0 / e[j][j]
            for m in range(j + 1, 8):
                l[m][j] = e[m][j] * inv[j]
            for m in range(j + 1, 8):
                for n in range(m, 8):
                    e[n][m] = e[n][m] - l[n][j] * e[m][j]
                u[m] = [a - l[m][j] * c for a, c in zip(u[m], u[j])]
        v = [[a * inv[j] for a in u[j]] for j in range(8)]
        for j in range(8):
            root = lax.rsqrt(e[j][j])
            root = root * (1.5 - 0.5 * e[j][j] * root * root)
            for t in range(wide // B):
                row = (u[j][t] * root)[0:1, :]
                if t < NB - p:
                    r_ref[lo + j : lo + j + 1, t * B : (t + 1) * B] = row
                else:
                    inv_ref[lo + j : lo + j + 1, :] = row
        for d in range(b + 1, B // 8):
            at = slice(8 * d, 8 * d + 8)
            tail = s_ref[at, :]
            cols = [jnp.broadcast_to(tail[:, lo + m : lo + m + 1], (8, B)) for m in range(8)]
            for j in range(8):
                for m in range(j + 1, 8):
                    cols[m] = cols[m] - cols[j] * l[m][j]
            for t in range(wide // B):
                x = tail[:, t * B : (t + 1) * B]
                y = cols[0] * v[0][t]
                z = cols[1] * v[1][t]
                for m in range(2, 8, 2):
                    y = y + cols[m] * v[m][t]
                    z = z + cols[m + 1] * v[m + 1][t]
                s_ref[at, t * B : (t + 1) * B] = x - (y + z)


def factor(p, me, near, far, prior):
    w = (NB - p) * B
    vm = pl.BlockSpec(memory_space=pltpu.VMEM)
    return pl.pallas_call(
        functools.partial(factor_kernel, p),
        out_shape=(
            jax.ShapeDtypeStruct((B, w), jnp.float32),
            jax.ShapeDtypeStruct((B, B), jnp.float32),
        ),
        in_specs=[pl.BlockSpec(memory_space=pltpu.SMEM)] + [vm] * (2 + p),
        out_specs=(vm, vm),
        scratch_shapes=[pltpu.VMEM((B, w + B), jnp.float32)],
        cost_estimate=pl.CostEstimate(flops=10_000_000_000, bytes_accessed=1 << 20, transcendentals=0),
    )(me, near, far, *prior)


def finish_kernel(w_ref, *refs):
    r, inv, x_ref = refs[:NB], refs[NB : 2 * NB], refs[2 * NB]
    for p in range(NB):
        acc = w_ref[:, p * B : (p + 1) * B]
        for q in range(p):
            acc = acc - lax.dot_general(
                x_ref[:, q * B : (q + 1) * B], r[q][:, (p - q) * B : (p - q + 1) * B],
                (((1,), (0,)), ((), ())), precision=HI, preferred_element_type=jnp.float32)
        x_ref[:, p * B : (p + 1) * B] = lax.dot_general(
            acc, inv[p][...], NT, precision=HI, preferred_element_type=jnp.float32)


def finish(owned, panels, inverses):
    vm = pl.BlockSpec(memory_space=pltpu.VMEM)
    return pl.pallas_call(
        finish_kernel,
        out_shape=jax.ShapeDtypeStruct(owned.shape, jnp.float32),
        in_specs=[vm] * (1 + 2 * NB),
        out_specs=vm,
        name="finish",
    )(owned, *panels, *inverses)


def shifted(value, axis, size, step):
    return lax.ppermute(value, axis, [(k, (k + step) % size) for k in range(size)])


def swap(value, axes):
    return lax.all_to_all(value, axes, 0, 0, tiled=True)


def copies(value, count):
    return jnp.broadcast_to(value[None], (count,) + value.shape)


def after(value, *others):
    return lax.optimization_barrier((value,) + others)


def steps(dosage, allele_freq, probes, owner_perm):
    c = lax.axis_index("c")
    me = jnp.full((1,), c, jnp.int32)
    mean_dose = (2.0 * allele_freq)[None, :]
    inv_spread = (1.0 / jnp.sqrt(2.0 * allele_freq * (1.0 - allele_freq)))[None, :]
    both, near, far = sketch_gram(me, dosage, mean_dose, inv_spread, probes)
    half = near + shifted(far, "c", NC, 1)
    half, both = after(half, both)
    part = swap(half.reshape(NX * NY, -1, B), ("x", "y"))
    rows = product(dosage, mean_dose, inv_spread, both)
    part, rows = after(part.sum(0), rows)
    part = swap(copies(part, NZ), "z")
    away = gather_rows(1, me, owner_perm, rows)
    part, away = after(part.sum(0), away)
    came = shifted(away, "c", NC, 1)
    near = swap(copies(part, NX * NY), ("x", "y")).reshape(-1, B)
    kept = gather_rows(0, me, owner_perm, rows, came)
    near, kept = after(near, kept)
    far = shifted(near, "c", NC, 1)
    k = rows.shape[1]
    owned = swap(kept.reshape(NX * NY, -1, k), ("x", "y"))
    panels, inverses = [], []
    for p in range(NB):
        r, inv = factor(p, me, near, far, panels)
        panels.append(r)
        inverses.append(inv)
    owned = owned.sum(0).reshape(NZ, -1, k)
    owned = swap(copies(owned, NX).reshape(NX * NZ, -1, k), ("x", "z"))
    owned = owned.reshape(NX, NZ, -1, k).sum(1).reshape(-1, k)
    return finish(owned, panels, inverses)


def solution(mesh):
    torus = Mesh(mesh.devices.reshape(NX, NZ, NY, NC), ("x", "z", "y", "c"))
    return jax.shard_map(
        steps,
        mesh=torus,
        in_specs=(P(("x", "z", "y", "c"), None), P(), P(), P()),
        out_specs=P(("z", "y", "c"), None),
        check_vma=False,
    )
```

```python
import functools

import jax
import jax.numpy as jnp
from jax import lax
from jax.experimental import pallas as pl
from jax.experimental.pallas import tpu as pltpu
from jax.sharding import Mesh, PartitionSpec as P


NX, NZ, NY, NC = 4, 8, 4, 2
B = 128
NB = 4
G8 = 8
PAIRS = [(i, j) for i in range(NB) for j in range(i, NB)]
HALF = len(PAIRS) // 2
ROWS = HALF * B // (NX * NY)

TN = (((0,), (0,)), ((), ()))


def dot(a, b, dims):
    return lax.dot_general(a, b, dims, preferred_element_type=jnp.float32)


def centre(d_ref, f_ref):
    freq = f_ref[...]
    scale = 1.0 / jnp.sqrt(2.0 * freq * (1.0 - freq))
    return ((d_ref[...].astype(jnp.float32) - 2.0 * freq) * scale).astype(jnp.bfloat16)


def sketch_kernel(me_ref, d_ref, f_ref, p_ref, hl_ref, packed_ref, a_ref):
    k = p_ref.shape[1]
    c = centre(d_ref, f_ref)
    sketch = jnp.dot(c, p_ref[...], preferred_element_type=jnp.float32)
    hi = sketch.astype(jnp.bfloat16)
    lo = (sketch - hi.astype(jnp.float32)).astype(jnp.bfloat16)
    hl_ref[:, :k] = hi
    hl_ref[:, k:] = lo
    i = pl.program_id(0)

    @pl.when(i == 0)
    def _():
        a_ref[...] = dot(hi, hl_ref[...], TN)

    @pl.when(i > 0)
    def _():
        a_ref[...] += dot(hi, hl_ref[...], TN)

    @pl.when(i == pl.num_programs(0) - 1)
    def _():
        def block(p, q):
            r, t = slice(p * B, (p + 1) * B), slice(q * B, (q + 1) * B)
            u, v = slice(k + p * B, k + (p + 1) * B), slice(k + q * B, k + (q + 1) * B)
            return a_ref[r, t] + (a_ref[r, v] + a_ref[t, u].T)

        first = me_ref[0] == 0
        for n in range(HALF):
            a, b = block(*PAIRS[n]), block(*PAIRS[n + HALF])
            near, far = jnp.where(first, a, b), jnp.where(first, b, a)
            for t in range(B // 8):
                chunk, row = divmod(n * (B // 8) + t, ROWS // 8)
                packed_ref[chunk, 8 * row : 8 * row + 8, :] = near[8 * t : 8 * t + 8]
                packed_ref[chunk, ROWS + 8 * row : ROWS + 8 * row + 8, :] = far[8 * t : 8 * t + 8]


def sketch_gram(me, dosage, freq, probes, step=512):
    n, m = dosage.shape
    k = probes.shape[1]
    whole = lambda i: (0, 0)
    return pl.pallas_call(
        sketch_kernel,
        grid=(n // step,),
        in_specs=[
            pl.BlockSpec(memory_space=pltpu.SMEM),
            pl.BlockSpec((step, m), lambda i: (i, 0)),
            pl.BlockSpec((1, m), whole),
            pl.BlockSpec((m, k), whole),
        ],
        out_specs=(
            pl.BlockSpec((step, 2 * k), lambda i: (i, 0)),
            pl.BlockSpec((NX * NY, NC * ROWS, B), lambda i: (0, 0, 0)),
        ),
        out_shape=(
            jax.ShapeDtypeStruct((n, 2 * k), jnp.bfloat16),
            jax.ShapeDtypeStruct((NX * NY, NC * ROWS, B), jnp.float32),
        ),
        scratch_shapes=[pltpu.VMEM((k, 2 * k), jnp.float32)],
        name="sketch_gram",
    )(me, dosage, freq, probes)


def product_kernel(d_ref, f_ref, hl_ref, w_ref):
    k = hl_ref.shape[1] // 2
    c = centre(d_ref, f_ref)
    both = dot(c, hl_ref[...], TN)
    for t in range(NB):
        at, below = slice(t * B, (t + 1) * B), slice(k + t * B, k + (t + 1) * B)
        w_ref[:, t, :] = both[:, at] + both[:, below]


def product(dosage, freq, hl, step=512):
    n, m = dosage.shape
    k = hl.shape[1] // 2
    return pl.pallas_call(
        product_kernel,
        grid=(m // step,),
        in_specs=[
            pl.BlockSpec((n, step), lambda i: (0, i)),
            pl.BlockSpec((1, step), lambda i: (0, i)),
            pl.BlockSpec((n, 2 * k), lambda i: (0, 0)),
        ],
        out_specs=pl.BlockSpec((step, NB, B), lambda i: (i, 0, 0)),
        out_shape=jax.ShapeDtypeStruct((m, NB, B), jnp.float32),
        name="product",
        cost_estimate=pl.CostEstimate(
            flops=4 * n * m * k, bytes_accessed=16 << 20, transcendentals=0
        ),
    )(dosage, freq, hl)


def gather_kernel(flip, me_ref, i_ref, w_ref, *refs):
    o_ref = refs[-1]
    c = (me_ref[0] + flip) & 1

    def block(n, _):
        base = 32 * ((n & 7) * (NY * NC) + ((n >> 3) & 3) * NC + c) + 8 * (n >> 5)
        for s in range(8):
            row = w_ref[i_ref[base + s]]
            o_ref[n * 8 + s] = row if flip else row + refs[0][n * 8 + s]
        return 0

    lax.fori_loop(0, NX * NY * NZ, block, 0, unroll=4)


def gather_rows(flip, me, perm, rows, *came):
    sm, vm = pl.BlockSpec(memory_space=pltpu.SMEM), pl.BlockSpec(memory_space=pltpu.VMEM)
    return pl.pallas_call(
        functools.partial(gather_kernel, flip),
        out_shape=jax.ShapeDtypeStruct((rows.shape[0] // NC,) + rows.shape[1:], rows.dtype),
        in_specs=[sm, sm, vm] + [vm] * len(came),
        out_specs=vm,
        cost_estimate=pl.CostEstimate(flops=6_000_000_000, bytes_accessed=8 << 20, transcendentals=0),
    )(me, perm, rows, *came)


HI = lax.Precision.HIGHEST
NT = (((1,), (1,)), ((), ()))


def factor_kernel(p, me_ref, near_ref, far_ref, *refs):
    prior = refs[:p]
    r_ref, inv_ref, s_ref = refs[p:]
    w = (NB - p) * B
    wide = w + B
    for t in range(NB - p):
        n = PAIRS.index((p, p + t))
        at = slice(n % HALF * B, (n % HALF + 1) * B)
        near = (n // HALF + me_ref[0]) & 1 == 0
        s_ref[:, t * B : (t + 1) * B] = jnp.where(near, near_ref[at, :], far_ref[at, :])
    for q in range(p):
        off = (p - q) * B
        s_ref[:, :w] -= lax.dot_general(
            prior[q][:, off : off + B], prior[q][:, off:], TN,
            precision=HI, preferred_element_type=jnp.float32)
    s_ref[:, w:] = (
        lax.broadcasted_iota(jnp.int32, (B, B), 0) == lax.broadcasted_iota(jnp.int32, (B, B), 1)
    ).astype(jnp.float32)
    ready = None
    for b in range(B // 8):
        lo = 8 * b
        if b and b % G8 == 0:
            done = slice(lo - 8 * G8, lo)
            lead = r_ref[done, :B]
            s_ref[lo:, :w] -= lax.dot_general(
                lead[:, lo:], r_ref[done, :], TN, precision=HI, preferred_element_type=jnp.float32)
            s_ref[lo:, w:] -= lax.dot_general(
                lead[:, lo:], inv_ref[done, :], TN, precision=HI, preferred_element_type=jnp.float32)
        rows = s_ref[lo : lo + 8, :] if ready is None else ready
        ready = None
        cols = [jnp.broadcast_to(rows[:, lo + m : lo + m + 1], (8, B)) for m in range(8)]
        e = [[jnp.broadcast_to(cols[m][j : j + 1, :], (8, B)) if j >= m else None
              for m in range(8)] for j in range(8)]
        u = [[jnp.broadcast_to(rows[j : j + 1, t * B : (t + 1) * B], (8, B))
              for t in range(wide // B)] for j in range(8)]
        inv = [None] * 8
        l = [[None] * 8 for _ in range(8)]
        for j in range(8):
            inv[j] = 1.0 / e[j][j]
            for m in range(j + 1, 8):
                l[m][j] = e[m][j] * inv[j]
            for m in range(j + 1, 8):
                for n in range(m, 8):
                    e[n][m] = e[n][m] - l[n][j] * e[m][j]
                u[m] = [a - l[m][j] * c for a, c in zip(u[m], u[j])]
        v = [[a * inv[j] for a in u[j]] for j in range(8)]
        for j in range(8):
            root = lax.rsqrt(e[j][j])
            root = root * (1.5 - 0.5 * e[j][j] * root * root)
            for t in range(wide // B):
                row = (u[j][t] * root)[0:1, :]
                if t < NB - p:
                    r_ref[lo + j : lo + j + 1, t * B : (t + 1) * B] = row
                else:
                    inv_ref[lo + j : lo + j + 1, :] = row
        for d in range(b + 1, (b // G8 + 1) * G8):
            at = slice(8 * d, 8 * d + 8)
            tail = s_ref[at, :]
            cols = [jnp.broadcast_to(tail[:, lo + m : lo + m + 1], (8, B)) for m in range(8)]
            for j in range(8):
                for m in range(j + 1, 8):
                    cols[m] = cols[m] - cols[j] * l[m][j]
            fresh = []
            for t in range(wide // B):
                x = tail[:, t * B : (t + 1) * B]
                y = cols[0] * v[0][t]
                z = cols[1] * v[1][t]
                for m in range(2, 8, 2):
                    y = y + cols[m] * v[m][t]
                    z = z + cols[m + 1] * v[m + 1][t]
                fresh.append(x - (y + z))
            if d == b + 1:
                ready = jnp.concatenate(fresh, axis=1)
            else:
                s_ref[at, :] = jnp.concatenate(fresh, axis=1)


def factor(p, me, near, far, prior):
    w = (NB - p) * B
    vm = pl.BlockSpec(memory_space=pltpu.VMEM)
    return pl.pallas_call(
        functools.partial(factor_kernel, p),
        out_shape=(
            jax.ShapeDtypeStruct((B, w), jnp.float32),
            jax.ShapeDtypeStruct((B, B), jnp.float32),
        ),
        in_specs=[pl.BlockSpec(memory_space=pltpu.SMEM)] + [vm] * (2 + p),
        out_specs=(vm, vm),
        scratch_shapes=[pltpu.VMEM((B, w + B), jnp.float32)],
        cost_estimate=pl.CostEstimate(flops=10_000_000_000, bytes_accessed=1 << 20, transcendentals=0),
    )(me, near, far, *prior)


def invert_kernel(*refs):
    r, inv, t_ref = refs[:NB], refs[NB : 2 * NB], refs[2 * NB]
    t_ref[...] = jnp.zeros_like(t_ref)
    for p in range(NB):
        at = slice(p * B, (p + 1) * B)
        t_ref[at, at] = inv[p][...].T
        if p:
            strip = jnp.concatenate(
                [r[k][:, (p - k) * B : (p - k + 1) * B] for k in range(p)], axis=0)
            strip = jnp.dot(t_ref[: p * B, : p * B], strip, precision=HI,
                            preferred_element_type=jnp.float32)
            t_ref[: p * B, at] = -lax.dot_general(
                strip, inv[p][...], NT, precision=HI, preferred_element_type=jnp.float32)


def invert(panels, inverses):
    vm = pl.BlockSpec(memory_space=pltpu.VMEM)
    return pl.pallas_call(
        invert_kernel,
        out_shape=jax.ShapeDtypeStruct((NB * B, NB * B), jnp.float32),
        in_specs=[vm] * (2 * NB),
        out_specs=vm,
        name="invert",
    )(*panels, *inverses)


def finish_kernel(w_ref, t_ref, x_ref, s_ref):
    n = x_ref.shape[0]
    rows = w_ref[:, 0]
    for z in range(1, w_ref.shape[1]):
        rows = rows + w_ref[:, z]
    s_ref[...] = rows.reshape(s_ref.shape)
    acc = None
    for t in range(NB):
        part = jnp.dot(s_ref[pl.ds(t, n, stride=NB), :], t_ref[t * B : (t + 1) * B, :],
                       precision=HI, preferred_element_type=jnp.float32)
        acc = part if acc is None else acc + part
    x_ref[...] = acc


def finish(parts, inverse):
    vm = pl.BlockSpec(memory_space=pltpu.VMEM)
    lines = parts.shape[0] * parts.shape[2]
    return pl.pallas_call(
        finish_kernel,
        out_shape=jax.ShapeDtypeStruct((lines // NB, NB * B), jnp.float32),
        in_specs=[vm] * 2,
        out_specs=vm,
        scratch_shapes=[pltpu.VMEM((lines, B), jnp.float32)],
        name="finish",
    )(parts, inverse)


def shifted(value, axis, size, step):
    return lax.ppermute(value, axis, [(k, (k + step) % size) for k in range(size)])


def swap(value, axes):
    return lax.all_to_all(value, axes, 0, 0, tiled=True)


def copies(value, count):
    return jnp.broadcast_to(value[None], (count,) + value.shape)


def after(value, *others):
    return lax.optimization_barrier((value,) + others)


def steps(dosage, allele_freq, probes, owner_perm):
    c = lax.axis_index("c")
    me = jnp.full((1,), c, jnp.int32)
    freq = allele_freq[None, :]
    both, packed = sketch_gram(me, dosage, freq, probes)
    part = swap(packed, ("x", "y"))
    rows = product(dosage, freq, both)
    part, rows = after(part.sum(0), rows)
    part = part[:ROWS] + shifted(part[ROWS:], "c", NC, 1)
    part = swap(copies(part, NZ), "z")
    away = gather_rows(1, me, owner_perm, rows)
    part, away = after(part.sum(0), away)
    came = shifted(away, "c", NC, 1)
    near = swap(copies(part, NX * NY), ("x", "y")).reshape(-1, B)
    kept = gather_rows(0, me, owner_perm, rows, came)
    near, kept = after(near, kept)
    far = shifted(near, "c", NC, 1)
    owned = swap(kept.reshape(NX * NY, -1, B), ("x", "y"))
    panels, inverses = [], []
    for p in range(NB):
        r, inv = factor(p, me, near, far, panels)
        panels.append(r)
        inverses.append(inv)
    owned = owned.sum(0).reshape(NZ, -1, B)
    owned = swap(copies(owned, NX).reshape(NX * NZ, -1, B), ("x", "z"))
    inverse = invert(panels, inverses)
    return finish(owned.reshape(NX, NZ, -1, B), inverse)


def solution(mesh):
    torus = Mesh(mesh.devices.reshape(NX, NZ, NY, NC), ("x", "z", "y", "c"))
    return jax.shard_map(
        steps,
        mesh=torus,
        in_specs=(P(("x", "z", "y", "c"), None), P(), P(), P()),
        out_specs=P(("z", "y", "c"), None),
        check_vma=False,
    )
```

```python
import functools

import jax
import jax.numpy as jnp
from jax import lax
from jax.experimental import pallas as pl
from jax.experimental.pallas import tpu as pltpu
from jax.sharding import Mesh, PartitionSpec as P


NX, NZ, NY, NC = 4, 8, 4, 2
B = 128
NB = 4
G8 = 8
PAIRS = [(i, j) for i in range(NB) for j in range(i, NB)]
HALF = len(PAIRS) // 2
ROWS = HALF * B // (NX * NY)

TN = (((0,), (0,)), ((), ()))


def dot(a, b, dims):
    return lax.dot_general(a, b, dims, preferred_element_type=jnp.float32)


def centre(d_ref, f_ref):
    freq = f_ref[...]
    scale = 1.0 / jnp.sqrt(2.0 * freq * (1.0 - freq))
    return ((d_ref[...].astype(jnp.float32) - 2.0 * freq) * scale).astype(jnp.bfloat16)


def sketch_kernel(me_ref, d_ref, f_ref, p_ref, hl_ref, packed_ref, a_ref):
    k = p_ref.shape[1]
    c = centre(d_ref, f_ref)
    sketch = jnp.dot(c, p_ref[...], preferred_element_type=jnp.float32)
    hi = sketch.astype(jnp.bfloat16)
    lo = (sketch - hi.astype(jnp.float32)).astype(jnp.bfloat16)
    hl_ref[:, :k] = hi
    hl_ref[:, k:] = lo
    i = pl.program_id(0)

    @pl.when(i == 0)
    def _():
        a_ref[...] = dot(hi, hl_ref[...], TN)

    @pl.when(i > 0)
    def _():
        a_ref[...] += dot(hi, hl_ref[...], TN)

    @pl.when(i == pl.num_programs(0) - 1)
    def _():
        def block(p, q):
            r, t = slice(p * B, (p + 1) * B), slice(q * B, (q + 1) * B)
            u, v = slice(k + p * B, k + (p + 1) * B), slice(k + q * B, k + (q + 1) * B)
            return a_ref[r, t] + (a_ref[r, v] + a_ref[t, u].T)

        first = me_ref[0] == 0
        for n in range(HALF):
            a, b = block(*PAIRS[n]), block(*PAIRS[n + HALF])
            near, far = jnp.where(first, a, b), jnp.where(first, b, a)
            for t in range(B // 8):
                chunk, row = divmod(n * (B // 8) + t, ROWS // 8)
                packed_ref[chunk, 8 * row : 8 * row + 8, :] = near[8 * t : 8 * t + 8]
                packed_ref[chunk, ROWS + 8 * row : ROWS + 8 * row + 8, :] = far[8 * t : 8 * t + 8]


def sketch_gram(me, dosage, freq, probes, step=512):
    n, m = dosage.shape
    k = probes.shape[1]
    whole = lambda i: (0, 0)
    return pl.pallas_call(
        sketch_kernel,
        grid=(n // step,),
        in_specs=[
            pl.BlockSpec(memory_space=pltpu.SMEM),
            pl.BlockSpec((step, m), lambda i: (i, 0)),
            pl.BlockSpec((1, m), whole),
            pl.BlockSpec((m, k), whole),
        ],
        out_specs=(
            pl.BlockSpec((step, 2 * k), lambda i: (i, 0)),
            pl.BlockSpec((NX * NY, NC * ROWS, B), lambda i: (0, 0, 0)),
        ),
        out_shape=(
            jax.ShapeDtypeStruct((n, 2 * k), jnp.bfloat16),
            jax.ShapeDtypeStruct((NX * NY, NC * ROWS, B), jnp.float32),
        ),
        scratch_shapes=[pltpu.VMEM((k, 2 * k), jnp.float32)],
        name="sketch_gram",
    )(me, dosage, freq, probes)


def product_kernel(d_ref, f_ref, hl_ref, w_ref):
    k = w_ref.shape[1]
    c = centre(d_ref, f_ref)
    both = dot(c, hl_ref[...], TN)
    w_ref[...] = both[:, :k] + both[:, k:]


def product(dosage, freq, hl, step=512):
    n, m = dosage.shape
    k = hl.shape[1] // 2
    return pl.pallas_call(
        product_kernel,
        grid=(m // step,),
        in_specs=[
            pl.BlockSpec((n, step), lambda i: (0, i)),
            pl.BlockSpec((1, step), lambda i: (0, i)),
            pl.BlockSpec((n, 2 * k), lambda i: (0, 0)),
        ],
        out_specs=pl.BlockSpec((step, k), lambda i: (i, 0)),
        out_shape=jax.ShapeDtypeStruct((m, k), jnp.float32),
        name="product",
        cost_estimate=pl.CostEstimate(
            flops=4 * n * m * k, bytes_accessed=16 << 20, transcendentals=0
        ),
    )(dosage, freq, hl)


def gather_kernel(flip, me_ref, i_ref, w_ref, *refs):
    o_ref = refs[-1]
    c = (me_ref[0] + flip) & 1

    def block(n, _):
        base = 32 * ((n & 7) * (NY * NC) + ((n >> 3) & 3) * NC + c) + 8 * (n >> 5)
        at = pl.ds(pl.multiple_of(n * 8, 8), 8)
        rows = jnp.concatenate([w_ref[pl.ds(i_ref[base + s], 1), :] for s in range(8)], axis=0)
        o_ref[at, :] = rows if flip else rows + refs[0][at, :]
        return 0

    lax.fori_loop(0, NX * NY * NZ, block, 0, unroll=4)


def gather_rows(flip, me, perm, rows, *came):
    sm, vm = pl.BlockSpec(memory_space=pltpu.SMEM), pl.BlockSpec(memory_space=pltpu.VMEM)
    return pl.pallas_call(
        functools.partial(gather_kernel, flip),
        out_shape=jax.ShapeDtypeStruct((rows.shape[0] // NC, rows.shape[1]), rows.dtype),
        in_specs=[sm, sm, vm] + [vm] * len(came),
        out_specs=vm,
        cost_estimate=pl.CostEstimate(flops=6_000_000_000, bytes_accessed=8 << 20, transcendentals=0),
    )(me, perm, rows, *came)


HI = lax.Precision.HIGHEST
NT = (((1,), (1,)), ((), ()))


def factor_kernel(p, me_ref, near_ref, far_ref, *refs):
    prior = refs[:p]
    r_ref, inv_ref, s_ref = refs[p:]
    w = (NB - p) * B
    wide = w + B
    for t in range(NB - p):
        n = PAIRS.index((p, p + t))
        at = slice(n % HALF * B, (n % HALF + 1) * B)
        near = (n // HALF + me_ref[0]) & 1 == 0
        s_ref[:, t * B : (t + 1) * B] = jnp.where(near, near_ref[at, :], far_ref[at, :])
    for q in range(p):
        off = (p - q) * B
        s_ref[:, :w] -= lax.dot_general(
            prior[q][:, off : off + B], prior[q][:, off:], TN,
            precision=HI, preferred_element_type=jnp.float32)
    s_ref[:, w:] = (
        lax.broadcasted_iota(jnp.int32, (B, B), 0) == lax.broadcasted_iota(jnp.int32, (B, B), 1)
    ).astype(jnp.float32)
    ready = None
    for b in range(B // 8):
        lo = 8 * b
        if b and b % G8 == 0:
            done = slice(lo - 8 * G8, lo)
            lead = r_ref[done, :B]
            s_ref[lo:, :w] -= lax.dot_general(
                lead[:, lo:], r_ref[done, :], TN, precision=HI, preferred_element_type=jnp.float32)
            s_ref[lo:, w:] -= lax.dot_general(
                lead[:, lo:], inv_ref[done, :], TN, precision=HI, preferred_element_type=jnp.float32)
        rows = s_ref[lo : lo + 8, :] if ready is None else ready
        ready = None
        cols = [jnp.broadcast_to(rows[:, lo + m : lo + m + 1], (8, B)) for m in range(8)]
        e = [[jnp.broadcast_to(cols[m][j : j + 1, :], (8, B)) if j >= m else None
              for m in range(8)] for j in range(8)]
        u = [[jnp.broadcast_to(rows[j : j + 1, t * B : (t + 1) * B], (8, B))
              for t in range(wide // B)] for j in range(8)]
        inv = [None] * 8
        l = [[None] * 8 for _ in range(8)]
        for j in range(8):
            inv[j] = 1.0 / e[j][j]
            for m in range(j + 1, 8):
                l[m][j] = e[m][j] * inv[j]
            for m in range(j + 1, 8):
                for n in range(m, 8):
                    e[n][m] = e[n][m] - l[n][j] * e[m][j]
                u[m] = [a - l[m][j] * c for a, c in zip(u[m], u[j])]
        v = [[a * inv[j] for a in u[j]] for j in range(8)]
        for j in range(8):
            root = lax.rsqrt(e[j][j])
            root = root * (1.5 - 0.5 * e[j][j] * root * root)
            for t in range(wide // B):
                row = (u[j][t] * root)[0:1, :]
                if t < NB - p:
                    r_ref[lo + j : lo + j + 1, t * B : (t + 1) * B] = row
                else:
                    inv_ref[lo + j : lo + j + 1, :] = row
        for d in range(b + 1, (b // G8 + 1) * G8):
            at = slice(8 * d, 8 * d + 8)
            tail = s_ref[at, :]
            cols = [jnp.broadcast_to(tail[:, lo + m : lo + m + 1], (8, B)) for m in range(8)]
            for j in range(8):
                for m in range(j + 1, 8):
                    cols[m] = cols[m] - cols[j] * l[m][j]
            fresh = []
            for t in range(wide // B):
                x = tail[:, t * B : (t + 1) * B]
                y = cols[0] * v[0][t]
                z = cols[1] * v[1][t]
                for m in range(2, 8, 2):
                    y = y + cols[m] * v[m][t]
                    z = z + cols[m + 1] * v[m + 1][t]
                fresh.append(x - (y + z))
            if d == b + 1:
                ready = jnp.concatenate(fresh, axis=1)
            else:
                s_ref[at, :] = jnp.concatenate(fresh, axis=1)


def factor(p, me, near, far, prior):
    w = (NB - p) * B
    vm = pl.BlockSpec(memory_space=pltpu.VMEM)
    return pl.pallas_call(
        functools.partial(factor_kernel, p),
        out_shape=(
            jax.ShapeDtypeStruct((B, w), jnp.float32),
            jax.ShapeDtypeStruct((B, B), jnp.float32),
        ),
        in_specs=[pl.BlockSpec(memory_space=pltpu.SMEM)] + [vm] * (2 + p),
        out_specs=(vm, vm),
        scratch_shapes=[pltpu.VMEM((B, w + B), jnp.float32)],
        cost_estimate=pl.CostEstimate(flops=10_000_000_000, bytes_accessed=1 << 20, transcendentals=0),
    )(me, near, far, *prior)


def invert_kernel(*refs):
    r, inv, t_ref = refs[:NB], refs[NB : 2 * NB], refs[2 * NB]
    t_ref[...] = jnp.zeros_like(t_ref)
    for p in range(NB):
        at = slice(p * B, (p + 1) * B)
        t_ref[at, at] = inv[p][...].T
        if p:
            strip = jnp.concatenate(
                [r[k][:, (p - k) * B : (p - k + 1) * B] for k in range(p)], axis=0)
            strip = jnp.dot(t_ref[: p * B, : p * B], strip, precision=HI,
                            preferred_element_type=jnp.float32)
            t_ref[: p * B, at] = -lax.dot_general(
                strip, inv[p][...], NT, precision=HI, preferred_element_type=jnp.float32)


def invert(panels, inverses):
    vm = pl.BlockSpec(memory_space=pltpu.VMEM)
    return pl.pallas_call(
        invert_kernel,
        out_shape=jax.ShapeDtypeStruct((NB * B, NB * B), jnp.float32),
        in_specs=[vm] * (2 * NB),
        out_specs=vm,
        name="invert",
    )(*panels, *inverses)


def finish_kernel(w_ref, t_ref, x_ref):
    rows = w_ref[:, 0]
    for z in range(1, w_ref.shape[1]):
        rows = rows + w_ref[:, z]
    x_ref[...] = jnp.dot(rows.reshape(x_ref.shape), t_ref[...], precision=HI,
                         preferred_element_type=jnp.float32)


def finish(parts, inverse):
    vm = pl.BlockSpec(memory_space=pltpu.VMEM)
    return pl.pallas_call(
        finish_kernel,
        out_shape=jax.ShapeDtypeStruct((parts.shape[0] * parts.shape[2], parts.shape[3]), jnp.float32),
        in_specs=[vm] * 2,
        out_specs=vm,
        name="finish",
    )(parts, inverse)


def shifted(value, axis, size, step):
    return lax.ppermute(value, axis, [(k, (k + step) % size) for k in range(size)])


def swap(value, axes):
    return lax.all_to_all(value, axes, 0, 0, tiled=True)


def copies(value, count):
    return jnp.broadcast_to(value[None], (count,) + value.shape)


def after(value, *others):
    return lax.optimization_barrier((value,) + others)


def steps(dosage, allele_freq, probes, owner_perm):
    c = lax.axis_index("c")
    me = jnp.full((1,), c, jnp.int32)
    freq = allele_freq[None, :]
    both, packed = sketch_gram(me, dosage, freq, probes)
    part = swap(packed, ("x", "y"))
    rows = product(dosage, freq, both)
    part, rows = after(part.sum(0), rows)
    part = part[:ROWS] + shifted(part[ROWS:], "c", NC, 1)
    part = swap(copies(part, NZ), "z")
    away = gather_rows(1, me, owner_perm, rows)
    part, away = after(part.sum(0), away)
    came = shifted(away, "c", NC, 1)
    near = swap(copies(part, NX * NY), ("x", "y")).reshape(-1, B)
    kept = gather_rows(0, me, owner_perm, rows, came)
    far = shifted(near, "c", NC, 1)
    k = rows.shape[1]
    owned = swap(kept.reshape(NX * NY, -1, k), ("x", "y"))
    panels, inverses = [], []
    for p in range(NB):
        r, inv = factor(p, me, near, far, panels)
        panels.append(r)
        inverses.append(inv)
    owned = owned.sum(0).reshape(NZ, -1, k)
    owned = swap(copies(owned, NX).reshape(NX * NZ, -1, k), ("x", "z"))
    inverse = invert(panels, inverses)
    return finish(owned.reshape(NX, NZ, -1, k), inverse)


def solution(mesh):
    torus = Mesh(mesh.devices.reshape(NX, NZ, NY, NC), ("x", "z", "y", "c"))
    return jax.shard_map(
        steps,
        mesh=torus,
        in_specs=(P(("x", "z", "y", "c"), None), P(), P(), P()),
        out_specs=P(("z", "y", "c"), None),
        check_vma=False,
    )
```
